32 devices in a mesh: row: 2 (over core), col: 4 (over y, x), depth: 4 (over z).
Axes of the slice: x: 2, y: 2, z: 4, core: 2. Of those that a mesh axis runs over, the one named last changes fastest.
Arguments:
- tokens: bfloat16 [1024, 8192], P(('col', 'depth'), 'row'), may hold values from -6 to 6
- out_grad: bfloat16 [1024, 8192], P(('col', 'depth'), 'row'), may hold values from -6 to 6
- gate_w: bfloat16 [8192, 14336], P('row', ('col', 'depth')), may hold values from -0.09375 to 0.09375
- up_w: bfloat16 [8192, 14336], P('row', ('col', 'depth')), may hold values from -0.09375 to 0.09375
- down_w: bfloat16 [14336, 8192], P(('col', 'depth'), 'row'), may hold values from -0.0625 to 0.0625
- keep_gate: int32 [64, 112], P('row', ('col', 'depth')), may hold values from 0 to 1, as said below
- keep_up: int32 [64, 112], P('row', ('col', 'depth')), may hold values from 0 to 1, as said below
- keep_down: int32 [112, 64], P(('col', 'depth'), 'row'), may hold values from 0 to 1, as said below
- exp_gate: int32 [64, 112], P('row', ('col', 'depth')), may hold values from -1 to 1
- exp_up: int32 [64, 112], P('row', ('col', 'depth')), may hold values from -1 to 1
- exp_down: int32 [112, 64], P(('col', 'depth'), 'row'), may hold values from -1 to 1
Outputs:
- output: bfloat16 [1024, 8192], P(('col', 'depth'), 'row')
- input_grad: bfloat16 [1024, 8192], P(('col', 'depth'), 'row')
- gate_w_grad: bfloat16 [8192, 14336], P('row', ('col', 'depth'))
- up_w_grad: bfloat16 [8192, 14336], P('row', ('col', 'depth'))
- down_w_grad: bfloat16 [14336, 8192], P(('col', 'depth'), 'row')
The draws below stay inside these ranges and needn't reach their ends.
Inputs may be any that keep to these rules, and one draw needn't show every extreme that they name: `keep_gate`: 1 where a weight block is kept, 0 where it is dropped; the share kept may differ from one block column to another. `keep_up`: 1 where a weight block is kept, 0 where it is dropped; the share kept may differ from one block column to another. `keep_down`: 1 where a weight block is kept, 0 where it is dropped; the share kept may differ from one block column to another.
All inputs are finite; a program needn't handle non-finite values.
Results may differ from the reference program's by a relative error of at most 0.005.
Values may be sent and summed in bfloat16 or wider, within the bound.
A program may use at most 256 MiB of HBM per device.

```python
import jax
import jax.numpy as jnp

D = 8192
FF = 14336
BLOCK = 128
TOKENS = 1024


def draw_blocks(key, rows, cols):
    level = jax.random.randint(jax.random.fold_in(key, 11), (1, cols), 1, 4)
    coin = jax.random.randint(jax.random.fold_in(key, 23), (rows, cols), 0, 4)
    return (coin < level).astype(jnp.int32)


def draw_keep_gate(key, part):
    return draw_blocks(jax.random.fold_in(key, 101), D // BLOCK, FF // BLOCK)


def draw_keep_up(key, part):
    return draw_blocks(jax.random.fold_in(key, 202), D // BLOCK, FF // BLOCK)


def draw_keep_down(key, part):
    return draw_blocks(jax.random.fold_in(key, 303), FF // BLOCK, D // BLOCK)


def set_ends(drawn, stream_key, smallest, largest):
    longest = drawn.shape.index(max(drawn.shape))
    spots = []
    for shift in (0, 1):
        where = [jax.random.randint(jax.random.fold_in(stream_key, axis), (), 0, length) for axis, length in enumerate(drawn.shape)]
        where[longest] = (where[longest] + shift) % drawn.shape[longest]
        spots.append(tuple(where))
    return drawn.at[spots[0]].set(smallest).at[spots[1]].set(largest)


def block_levels(stream_key, shape, pieces, least, high):
    def one(axis_at, parts):
        steps = jax.random.uniform(jax.random.fold_in(jax.random.fold_in(stream_key, 6), axis_at), (parts,), jnp.float32, least / len(pieces), high / len(pieces))
        return jnp.repeat(jnp.exp(steps), shape[axis_at] // parts).reshape((-1,) + (1,) * (len(shape) - axis_at - 1))

    level = one(*pieces[0])
    for cut in pieces[1:]:
        level = level * one(*cut)
    return level


def noise(own_key, shape, spread, most, cuts=(), kind=jnp.bfloat16):
    drawn = jax.random.normal(own_key, shape, jnp.float32) * spread
    if len(cuts) > 0:
        drawn = block_levels(own_key, shape, cuts, -0.22, 0.18) * drawn
    return jnp.clip(drawn, min=-most, max=most).astype(kind)


def setup_inputs(seed: int = 0) -> dict:
    key_list = jax.random.split(jax.random.key(seed), 12)
    return {
        "tokens": noise(key_list[0], (TOKENS, D), 1.0, 6.0, ((0, 16), (1, 2))),
        "out_grad": noise(key_list[1], (TOKENS, D), 1.0, 6.0, ((0, 16), (1, 2))),
        "gate_w": noise(key_list[2], (D, FF), (D // 2) ** -0.5, 0.09375, ((0, 2), (1, 16))),
        "up_w": noise(key_list[3], (D, FF), (D // 2) ** -0.5, 0.09375, ((0, 2), (1, 16))),
        "down_w": noise(key_list[4], (FF, D), (FF // 2) ** -0.5, 0.0625, ((0, 16), (1, 2))),
        "keep_gate": draw_keep_gate(jax.random.fold_in(key_list[11], 71), 0),
        "keep_up": draw_keep_up(jax.random.fold_in(key_list[11], 71), 0),
        "keep_down": draw_keep_down(jax.random.fold_in(key_list[11], 71), 0),
        "exp_gate": set_ends(jax.random.randint(key_list[8], (D // BLOCK, FF // BLOCK), -1, 2), jax.random.fold_in(key_list[8], 1), -1, 1).astype(jnp.int32),
        "exp_up": set_ends(jax.random.randint(key_list[9], (D // BLOCK, FF // BLOCK), -1, 2), jax.random.fold_in(key_list[9], 1), -1, 1).astype(jnp.int32),
        "exp_down": set_ends(jax.random.randint(key_list[10], (FF // BLOCK, D // BLOCK), -1, 2), jax.random.fold_in(key_list[10], 1), -1, 1).astype(jnp.int32),
    }


def block_factor(keep, exps):
    return keep.astype(jnp.float32) * jnp.exp2(exps.astype(jnp.float32))

def scaled(raw, factor):
    rows, cols = factor.shape
    high = raw.shape[0] // rows
    wide = raw.shape[1] // cols
    blocks = raw.reshape(rows, high, cols, wide) * factor.astype(jnp.bfloat16)[:, None, :, None]
    return blocks.reshape(raw.shape)

def masked_grad(grad, factor):
    rows, cols = factor.shape
    blocks = grad.reshape(rows, grad.shape[0] // rows, cols, grad.shape[1] // cols) * factor[:, None, :, None]
    return blocks.reshape(grad.shape).astype(jnp.bfloat16)

def reference(tokens, out_grad, gate_w, up_w, down_w, keep_gate, keep_up, keep_down, exp_gate, exp_up, exp_down):
    factor_gate = block_factor(keep_gate, exp_gate)
    factor_up = block_factor(keep_up, exp_up)
    factor_down = block_factor(keep_down, exp_down)
    eff_gate = scaled(gate_w, factor_gate)
    eff_up = scaled(up_w, factor_up)
    eff_down = scaled(down_w, factor_down)
    gate = jnp.dot(tokens, eff_gate, preferred_element_type=jnp.float32)
    up = jnp.dot(tokens, eff_up, preferred_element_type=jnp.float32)
    hidden_grad = jnp.dot(out_grad, eff_down.T, preferred_element_type=jnp.float32)
    sig = jax.nn.sigmoid(gate)
    hidden = (gate * sig * up).astype(jnp.bfloat16)
    output = jnp.dot(hidden, eff_down, preferred_element_type=jnp.float32).astype(jnp.bfloat16)
    gate_grad = (hidden_grad * up * sig * (1.0 + gate * (1.0 - sig))).astype(jnp.bfloat16)
    up_grad = (hidden_grad * gate * sig).astype(jnp.bfloat16)
    input_grad = (jnp.dot(gate_grad, eff_gate.T, preferred_element_type=jnp.float32) + jnp.dot(up_grad, eff_up.T, preferred_element_type=jnp.float32)).astype(jnp.bfloat16)
    gate_w_grad = masked_grad(jnp.dot(tokens.T, gate_grad, preferred_element_type=jnp.float32), factor_gate)
    up_w_grad = masked_grad(jnp.dot(tokens.T, up_grad, preferred_element_type=jnp.float32), factor_up)
    down_w_grad = masked_grad(jnp.dot(hidden.T, out_grad, preferred_element_type=jnp.float32), factor_down)
    return (output, input_grad, gate_w_grad, up_w_grad, down_w_grad)
```

```python
import jax
import jax.numpy as jnp
from jax import lax
from jax.sharding import PartitionSpec as P


def block_factor(keep, exps):
    return keep.astype(jnp.float32) * jnp.exp2(exps.astype(jnp.float32))


def scaled(raw, factor):
    rows, cols = factor.shape
    high = raw.shape[0] // rows
    wide = raw.shape[1] // cols
    blocks = raw.reshape(rows, high, cols, wide) * factor.astype(jnp.bfloat16)[:, None, :, None]
    return blocks.reshape(raw.shape)


def masked_grad(grad, factor):
    rows, cols = factor.shape
    blocks = (
        grad.reshape(rows, grad.shape[0] // rows, cols, grad.shape[1] // cols)
        * factor[:, None, :, None]
    )
    return blocks.reshape(grad.shape).astype(jnp.bfloat16)


def activate(gate, up, hidden_grad):
    sig = jax.nn.sigmoid(gate)
    hidden = (gate * sig * up).astype(jnp.bfloat16)
    gate_grad = (hidden_grad * up * sig * (1.0 + gate * (1.0 - sig))).astype(jnp.bfloat16)
    up_grad = (hidden_grad * gate * sig).astype(jnp.bfloat16)
    return (hidden, gate_grad, up_grad)


def halve(part, axis, bit, index):
    size = lax.axis_size(axis)
    mine = (index >> bit) & 1
    give = lax.dynamic_index_in_dim(part, 1 - mine, 0, keepdims=False).astype(jnp.bfloat16)
    keep = lax.dynamic_index_in_dim(part, mine, 0, keepdims=False)
    got = lax.ppermute(give, axis, [(i, i ^ (1 << bit)) for i in range(size)])
    return keep.astype(jnp.float32) + got.astype(jnp.float32)


def line_scatter(part, axis):
    size = lax.axis_size(axis)
    index = lax.axis_index(axis)
    up = down = None
    for step in range(size - 1):
        far = size - 1 - step
        above = lax.dynamic_index_in_dim(part, jnp.minimum(index + far, size - 1), 0, keepdims=False)
        below = lax.dynamic_index_in_dim(part, jnp.maximum(index - far, 0), 0, keepdims=False)
        if step:
            above, below = (above + up.astype(jnp.float32), below + down.astype(jnp.float32))
        up = lax.ppermute(above.astype(jnp.bfloat16), axis, [(i, i + 1) for i in range(size - far)])
        down = lax.ppermute(below.astype(jnp.bfloat16), axis, [(i, i - 1) for i in range(far, size)])
    total = lax.dynamic_index_in_dim(part, index, 0, keepdims=False)
    if up is not None:
        total = total + up.astype(jnp.float32) + down.astype(jnp.float32)
    return total


def scatter_sum(part, low_first):
    cols, depths = lax.axis_size("col"), lax.axis_size("depth")
    rows, wide = part.shape
    if cols & (cols - 1):
        return lax.psum_scatter(
            part.astype(jnp.float32), ("col", "depth"), scatter_dimension=0, tiled=True
        )
    bits = list(range(cols.bit_length() - 1))
    part = part.reshape((2,) * len(bits) + (depths, rows // (cols * depths), wide))
    index = lax.axis_index("col")
    left = bits[::-1]
    for bit in bits if low_first else bits[::-1]:
        at = left.index(bit)
        part = halve(jnp.moveaxis(part, at, 0), "col", bit, index)
        left.pop(at)
    return line_scatter(part.astype(jnp.float32), "depth")


def scatter_halves(part):
    half = part.shape[1] // 2
    return jnp.concatenate(
        [
            scatter_sum(part[:, :half], True).astype(jnp.bfloat16),
            scatter_sum(part[:, half:], False).astype(jnp.bfloat16),
        ],
        axis=1,
    )


def shards(
    tokens,
    out_grad,
    gate_w,
    up_w,
    down_w,
    keep_gate,
    keep_up,
    keep_down,
    exp_gate,
    exp_up,
    exp_down,
):
    factor_gate = block_factor(keep_gate, exp_gate)
    factor_up = block_factor(keep_up, exp_up)
    factor_down = block_factor(keep_down, exp_down)
    eff_gate = scaled(gate_w, factor_gate)
    eff_up = scaled(up_w, factor_up)
    eff_down = scaled(down_w, factor_down)
    width = gate_w.shape[1]
    paired = jnp.concatenate([eff_gate, eff_up], axis=1)
    gathered_in, gathered_grad = (
        lax.all_gather(tokens, ("col", "depth"), axis=0, tiled=True),
        lax.all_gather(out_grad, ("col", "depth"), axis=0, tiled=True),
    )
    sums = lax.psum_scatter(
        jnp.concatenate(
            [
                jnp.dot(gathered_in, paired, preferred_element_type=jnp.float32),
                jnp.dot(gathered_grad, eff_down.T, preferred_element_type=jnp.float32),
            ],
            axis=1,
        ),
        "row",
        scatter_dimension=0,
        tiled=True,
    )
    hidden, gate_grad, up_grad = activate(
        sums[:, :width], sums[:, width : 2 * width], sums[:, 2 * width :]
    )
    whole = lax.all_gather(
        jnp.concatenate([hidden, gate_grad, up_grad], axis=1), "row", axis=0, tiled=True
    )
    hidden_all = whole[:, :width]
    pair_grad = whole[:, width:]
    output = scatter_halves(
        jnp.dot(hidden_all, eff_down, preferred_element_type=jnp.float32).astype(jnp.bfloat16)
    )
    input_grad = scatter_halves(
        jnp.dot(pair_grad, paired.T, preferred_element_type=jnp.float32).astype(jnp.bfloat16)
    )
    pair_weights = jnp.dot(gathered_in.T, pair_grad, preferred_element_type=jnp.float32)
    gate_w_grad = masked_grad(pair_weights[:, :width], factor_gate)
    up_w_grad = masked_grad(pair_weights[:, width:], factor_up)
    down_w_grad = masked_grad(
        jnp.dot(hidden_all.T, gathered_grad, preferred_element_type=jnp.float32), factor_down
    )
    return (output, input_grad, gate_w_grad, up_w_grad, down_w_grad)


def solution(mesh):
    return jax.shard_map(
        shards,
        mesh=mesh,
        in_specs=(
            P(("col", "depth"), "row"),
            P(("col", "depth"), "row"),
            P("row", ("col", "depth")),
            P("row", ("col", "depth")),
            P(("col", "depth"), "row"),
            P("row", ("col", "depth")),
            P("row", ("col", "depth")),
            P(("col", "depth"), "row"),
            P("row", ("col", "depth")),
            P("row", ("col", "depth")),
            P(("col", "depth"), "row"),
        ),
        out_specs=(
            P(("col", "depth"), "row"),
            P(("col", "depth"), "row"),
            P("row", ("col", "depth")),
            P("row", ("col", "depth")),
            P(("col", "depth"), "row"),
        ),
        check_vma=False,
    )
```
